32 devices in a mesh: fsdp: 4 (over y, core), ctx: 8 (over z, x).
Axes of the slice: x: 2, y: 2, z: 4, core: 2. Of those that a mesh axis runs over, the one named last changes fastest.
Arguments:
- inputs: bfloat16 [4, 2048, 768], P('fsdp', 'ctx'), may hold values from -6 to 6
- cotangent: bfloat16 [4, 2048, 768], P('fsdp', 'ctx'), may hold values from -6 to 6
- norm1_gain: bfloat16 [768], P('fsdp'), may hold values from 0.25 to 1.75
- qkv_weight: bfloat16 [768, 2304], P('fsdp'), may hold values from -0.21875 to 0.21875
- out_weight: bfloat16 [768, 768], P('fsdp'), may hold values from -6 to 6
- norm2_gain: bfloat16 [768], P('fsdp'), may hold values from 0.25 to 1.75
- gate_up_weight: bfloat16 [768, 2304], P('fsdp'), may hold values from -0.21875 to 0.21875
- down_weight: bfloat16 [1152, 768], P(None, 'fsdp'), may hold values from -0.1875 to 0.1875
Outputs:
- output: bfloat16 [4, 2048, 768], P('fsdp', 'ctx')
- input_grad: float32 [4, 2048, 768], P('fsdp', 'ctx')
- norm1_gain_grad: float32 [768], P('fsdp')
- norm2_gain_grad: float32 [768], P('fsdp')
- qkv_weight_grad: float32 [768, 2304], P('fsdp')
- out_weight_grad: float32 [768, 768], P('fsdp')
- gate_up_weight_grad: float32 [768, 2304], P('fsdp')
- down_weight_grad: float32 [1152, 768], P(None, 'fsdp')
The draws below stay inside these ranges and needn't reach their ends.
All inputs are finite; a program needn't handle non-finite values.
Results may differ from the reference program's by a relative error of at most 0.017.
Values may be sent and summed in bfloat16 or wider, within the bound.
A program may use at most 384 MiB of HBM per device.

```python
import math
import jax
import jax.numpy as jnp
from jax import lax

D = 768
HEADS = 12
HEAD_DIM = 64
FF = 1152
LENGTH = 2048
SEQUENCES = 4


def levels(stream_key, dims, shards, smallest, high):
    def one(axis_at, parts):
        heights = jax.random.uniform(jax.random.fold_in(jax.random.fold_in(stream_key, 6), axis_at), (parts,), jnp.float32, smallest / len(shards), high / len(shards))
        return jnp.repeat(jnp.exp(heights), dims[axis_at] // parts).reshape((-1,) + (1,) * (len(dims) - axis_at - 1))

    gain = one(*shards[0])
    for cut in shards[1:]:
        gain = gain * one(*cut)
    return gain


def noise(own_key, dims, width, bound, cuts=(), kind=jnp.bfloat16):
    array = jax.random.normal(own_key, dims, jnp.float32) * width
    if len(cuts) > 0:
        array = levels(own_key, dims, cuts, -0.22, 0.18) * array
    return jnp.clip(array, min=-bound, max=bound).astype(kind)


def setup_inputs(seed: int = 0) -> dict:
    keys = jax.random.split(jax.random.key(seed), 9)
    inputs = noise(keys[0], (SEQUENCES, LENGTH, D), 1.0, 6.0, ((0, 4), (1, 8)))
    cotangent = noise(keys[1], (SEQUENCES, LENGTH, D), 1.0, 6.0, ((0, 4), (1, 8)))
    norm1_gain = jnp.clip(1.0 + 0.15 * jax.random.normal(keys[2], (D,), jnp.float32), 0.25, 1.75).astype(jnp.bfloat16)
    qkv_weight = noise(keys[3], (D, 3 * D), D ** -0.5, 0.21875, ((0, 4),))
    out_weight = noise(keys[4], (D, D), (max(1, 4 * D // LENGTH)) ** -0.5, 6.0, ((0, 4),))
    norm2_gain = jnp.clip(1.0 + 0.15 * jax.random.normal(keys[5], (D,), jnp.float32), 0.25, 1.75).astype(jnp.bfloat16)
    gate_up_weight = noise(keys[6], (D, 2 * FF), D ** -0.5, 0.21875, ((0, 4),))
    down_weight = noise(keys[7], (FF, D), FF ** -0.5, 0.1875, ((1, 4),))
    return {"inputs": inputs, "cotangent": cotangent, "norm1_gain": norm1_gain, "qkv_weight": qkv_weight, "out_weight": out_weight, "norm2_gain": norm2_gain, "gate_up_weight": gate_up_weight, "down_weight": down_weight}


@jax.custom_vjp
def low(v):
    return lax.optimization_barrier(v.astype(jnp.bfloat16)).astype(jnp.float32)

@jax.custom_vjp
def low_back(v):
    return v

def low_keep(v):
    return (low(v), None)

def low_pass(kept, grad):
    return (grad,)

def back_keep(v):
    return (v, None)

def back_low(kept, grad):
    return (low(grad),)
low.defvjp(low_keep, low_pass)
low_back.defvjp(back_keep, back_low)
highest = lax.Precision.HIGHEST

def layer_norm(values, norm_gain):
    center = values - lax.optimization_barrier(jnp.mean(values, axis=-1, keepdims=True))
    spread = lax.optimization_barrier(jnp.mean(center * center, axis=-1, keepdims=True))
    return center * lax.rsqrt(spread + 1e-05) * norm_gain

def rotate(values, cosine_table, sine_table):
    half_size = values.shape[-1] // 2
    leading = values[..., :half_size]
    trailing = values[..., half_size:]
    return jnp.concatenate([leading * cosine_table - trailing * sine_table, trailing * cosine_table + leading * sine_table], axis=-1)

def rope_tables(positions):
    indices = jnp.arange(HEAD_DIM // 2).astype(jnp.float32)
    frequency = jnp.exp(indices * (-2.0 * math.log(160000.0) / HEAD_DIM))
    angles = positions[:, None] * frequency[None, :]
    return (jnp.cos(angles)[:, None, :], jnp.sin(angles)[:, None, :])

def gelu_exact(values):
    return 0.5 * values * (1.0 + jax.scipy.special.erf(values * 0.7071067811865476))

def attention(queries, key_rows, value_rows):
    row_count = math.gcd(LENGTH, 512)

    def attend_block(block_rows):
        scores = low_back(jnp.einsum('qhe,khe->hqk', block_rows, key_rows, precision=highest))
        shifted = scores - lax.optimization_barrier(jnp.max(scores, axis=-1, keepdims=True))
        expd = jnp.exp(shifted)
        probabilities = expd / lax.optimization_barrier(jnp.sum(expd, axis=-1, keepdims=True))
        return jnp.einsum('hqk,khe->qhe', low(probabilities), value_rows, precision=highest)
    stacked = queries.reshape(LENGTH // row_count, row_count, HEADS, HEAD_DIM)
    return lax.map(jax.checkpoint(attend_block), stacked).reshape(LENGTH, D)

def forward(tokens, gain_one, w_qkv, w_out, gain_two, w_gate_up, w_down, cosine_table, sine_table):
    normed = low(layer_norm(tokens, gain_one))
    projected = low_back(jnp.dot(normed, w_qkv, precision=highest))
    heads_view = projected.reshape(LENGTH, 3, HEADS, HEAD_DIM)
    queries = low(low_back(rotate(heads_view[:, 0], cosine_table, sine_table) * 0.125))
    key_rows = low(low_back(rotate(heads_view[:, 1], cosine_table, sine_table)))
    value_rows = low(low_back(heads_view[:, 2]))
    attended = low(low_back(attention(queries, key_rows, value_rows)))
    middle = tokens + low_back(jnp.dot(attended, w_out, precision=highest))
    normed_two = low(layer_norm(middle, gain_two))
    gate_up = low_back(jnp.dot(normed_two, w_gate_up, precision=highest))
    hidden = low(gelu_exact(gate_up[:, :FF]) * gate_up[:, FF:])
    return middle + low_back(jnp.dot(hidden, w_down, precision=highest))

def reference(inputs, cotangent, norm1_gain, qkv_weight, out_weight, norm2_gain, gate_up_weight, down_weight):
    weights_in = tuple((weight_one.astype(jnp.float32) for weight_one in (norm1_gain, qkv_weight, out_weight, norm2_gain, gate_up_weight, down_weight)))
    positions = jnp.arange(LENGTH).astype(jnp.float32)
    cosine_table, sine_table = rope_tables(positions)

    def apply_layer(tokens, gain_one, w_qkv, w_out, gain_two, w_gate_up, w_down):
        return forward(tokens, gain_one, w_qkv, w_out, gain_two, w_gate_up, w_down, cosine_table, sine_table)

    def per_sequence(totals, record):
        sequence, tangent = record
        result, pullback = jax.vjp(apply_layer, sequence, *weights_in)
        gradients = pullback(tangent)
        totals = tuple((total_one + grad_one for total_one, grad_one in zip(totals, gradients[1:])))
        return (totals, (result.astype(jnp.bfloat16), gradients[0]))
    started = tuple((jnp.zeros_like(weight_one) for weight_one in weights_in))
    totals, outputs = lax.scan(per_sequence, started, (inputs.astype(jnp.float32), cotangent.astype(jnp.float32)))
    return (outputs[0], outputs[1], totals[0], totals[3], totals[1], totals[2], totals[4], totals[5])
```

```python
import math

import jax
import jax.numpy as jnp
from jax import lax
from jax.experimental import pallas as pl
from jax.experimental.pallas import tpu as pltpu
from jax.sharding import PartitionSpec as P

D = 768
HEADS = 12
HEAD_DIM = 64
FF = 1152


def layer_norm(values, norm_gain):
    center = values - jnp.mean(values, axis=-1, keepdims=True)
    spread = jnp.mean(center * center, axis=-1, keepdims=True)
    return center * lax.rsqrt(spread + 1e-05) * norm_gain


def rotate(values, cosine_table, sine_table):
    half_size = values.shape[-1] // 2
    leading = values[..., :half_size]
    trailing = values[..., half_size:]
    return jnp.concatenate(
        [
            leading * cosine_table - trailing * sine_table,
            trailing * cosine_table + leading * sine_table,
        ],
        axis=-1,
    )


def rope_tables(positions):
    indices = jnp.arange(HEAD_DIM // 2).astype(jnp.float32)
    frequency = jnp.exp(indices * (-2.0 * math.log(160000.0) / HEAD_DIM))
    angles = positions[:, None] * frequency[None, :]
    return (jnp.cos(angles)[:, None, :], jnp.sin(angles)[:, None, :])


def gelu_exact(values):
    return 0.5 * values * (1.0 + jax.scipy.special.erf(values * 0.7071067811865476))


def geglu(gate_up):
    return gelu_exact(gate_up[:, :FF]) * gate_up[:, FF:]


def split_rope(projected, cosine_table, sine_table):
    heads_view = projected.reshape(projected.shape[0], 3, HEADS, HEAD_DIM)
    return (
        rotate(heads_view[:, 0], cosine_table, sine_table) * 0.125,
        rotate(heads_view[:, 1], cosine_table, sine_table),
        heads_view[:, 2],
    )


def heads_of(flat_rows):
    return flat_rows.reshape(flat_rows.shape[0], HEADS, HEAD_DIM)


def rounded(values):
    return lax.optimization_barrier(values.astype(jnp.bfloat16)).astype(jnp.float32)


def by_blocks(pieces, carry, visit):
    row_count = pieces[0].shape[0]
    block_size = math.gcd(row_count, 2048)
    stacked = tuple(
        (
            piece_rows.reshape((row_count // block_size, block_size) + piece_rows.shape[1:])
            for piece_rows in pieces
        )
    )

    def step_block(running, record):
        number, block_parts = record
        return (visit(running, block_parts, number * block_size), None)

    running, _ = lax.scan(
        step_block, carry, (jnp.arange(row_count // block_size, dtype=jnp.int32), stacked)
    )
    return running


def score_parts(query_block, key_block, value_block, grad_block, log_block, delta_block):
    scores = jnp.einsum("qhe,khe->hqk", query_block, key_block, preferred_element_type=jnp.float32)
    probabilities = jnp.exp(scores - log_block[:, :, None])
    grad_probs = jnp.einsum(
        "qhe,khe->hqk", grad_block, value_block, preferred_element_type=jnp.float32
    )
    grad_scores = (probabilities * (grad_probs - delta_block[:, :, None])).astype(jnp.bfloat16)
    return (probabilities.astype(jnp.bfloat16), grad_scores)


MESH = pl.DeviceIdType.MESH
ANY = pl.BlockSpec(memory_space=pl.ANY)
WHOLE = pl.BlockSpec(memory_space=pltpu.VMEM)


def ring_neighbours():
    n = lax.axis_size("ctx")
    index = lax.axis_index("ctx")
    odd = index % 2
    place = (1 - odd) * (index // 2) + odd * (n - 1 - index // 2)

    def index_of(position):
        upper = position // (n // 2)
        return (1 - upper) * 2 * position + upper * (2 * (n - 1 - position) + 1)

    return index_of((place + 1) % n), index_of((place + n - 1) % n)


def send_to(source, target, send_sem, recv_sem, index):
    return pltpu.make_async_remote_copy(
        src_ref=source,
        dst_ref=target,
        send_sem=send_sem,
        recv_sem=recv_sem,
        device_id={"ctx": index},
        device_id_type=MESH,
    )


def greet(neighbours):
    barrier = pltpu.get_barrier_semaphore()
    for index in neighbours:
        pl.semaphore_signal(barrier, inc=1, device_id={"ctx": index}, device_id_type=MESH)
    pl.semaphore_wait(barrier, 2)


def gather_kernel(n, own, slots, local_sem, send_sem, recv_sem):
    ahead, behind = ring_neighbours()
    half = own.shape[0] // 2
    greet((ahead, behind))
    keep = pltpu.make_async_copy(own, slots.at[0], local_sem)
    keep.start()
    parts = (pl.ds(0, half), pl.ds(half, half))

    def copies(step, way):
        found = []
        for part in (0, 1):
            if step == n // 2 - 1 and part != way:
                continue
            here, there = (step, step + 1) if way == 0 else ((n - step) % n, n - step - 1)
            source = own if step == 0 else slots.at[here]
            found.append(
                send_to(
                    source.at[parts[part]],
                    slots.at[there, parts[part]],
                    send_sem.at[way, step, part],
                    recv_sem.at[way, step, part],
                    (ahead, behind)[way],
                )
            )
        return found

    steps = n // 2
    made = {}
    for step in range(steps):
        for part in (0, 1):
            for way in (0, 1):
                last = step == steps - 1
                if last and part != way:
                    continue
                if step > 0:
                    made[step - 1, way][part].wait_recv()
                if part == 0 or last:
                    made[step, way] = copies(step, way)
                copy = made[step, way][0 if last else part]
                copy.start()
    for way in (0, 1):
        if steps > 1:
            made[steps - 2, way][1 - way].wait_recv()
        made[steps - 1, way][0].wait_recv()
    for key in made:
        for copy in made[key]:
            copy.wait_send()
    keep.wait()


def ring_gather(block):
    n = lax.axis_size("ctx")
    rows, columns = block.shape
    return pl.pallas_call(
        lambda *refs: gather_kernel(n, *refs),
        out_shape=jax.ShapeDtypeStruct((n, rows, columns), block.dtype),
        in_specs=[WHOLE],
        out_specs=ANY,
        scratch_shapes=[
            pltpu.SemaphoreType.DMA,
            pltpu.SemaphoreType.DMA((2, n // 2, 2)),
            pltpu.SemaphoreType.DMA((2, n // 2, 2)),
        ],
        cost_estimate=pl.CostEstimate(
            flops=70_000_000_000, bytes_accessed=2 * n * block.size, transcendentals=0
        ),
        compiler_params=pltpu.CompilerParams(collective_id=1, has_side_effects=True),
        name="ring_gather",
    )(block)


def scatter_kernel(n, terms, total, landed, staged, load_sem, send_sem, recv_sem):
    ahead, behind = ring_neighbours()
    half = total.shape[1] // 2
    parts = (pl.ds(0, half), pl.ds(half, half))

    def load(step, way):
        slot = (step + 1) % n if way == 0 else (2 * n - step - 1) % n
        return pltpu.make_async_copy(
            terms.at[way, slot], staged.at[way, step % 2], load_sem.at[way, step % 2]
        )

    for way in (0, 1):
        load(0, way).start()
    for way in (0, 1):
        load(1, way).start()
    greet((ahead, behind))
    made = {}

    def send(step, way, part):
        source = staged.at[way, 0] if step == 0 else landed.at[way, step - 1]
        copy = send_to(
            source.at[parts[part]],
            landed.at[way, step, parts[part]],
            send_sem.at[way, step, part],
            recv_sem.at[way, step, part],
            (ahead, behind)[way],
        )
        copy.start()
        made[step, way, part] = copy

    for way in (0, 1):
        load(0, way).wait()
        for part in (0, 1):
            send(0, way, part)
    for step in range(1, n):
        for way in (0, 1):
            load(step, way).wait()
        for part in (0, 1):
            for way in (0, 1):
                made[step - 1, way, part].wait_recv()
                rows = parts[part]
                summed = landed[way, step - 1, rows].astype(jnp.float32) + staged[
                    way, step % 2, rows
                ].astype(jnp.float32)
                if step == n - 1:
                    total[way, rows] = summed.astype(total.dtype)
                else:
                    landed[way, step - 1, rows] = summed.astype(landed.dtype)
                    send(step, way, part)
        if step + 1 < n:
            for way in (0, 1):
                if step == 1:
                    for part in (0, 1):
                        made[0, way, part].wait_send()
                if step >= 1 and step + 1 < n:
                    load(step + 1, way).start()
    for key in made:
        if key[0] > 0:
            made[key].wait_send()


def ring_scatter(terms, kind, ident):
    _, n, rows, columns = terms.shape
    return pl.pallas_call(
        lambda *refs: scatter_kernel(n, *refs),
        out_shape=jax.ShapeDtypeStruct((2, rows, columns), kind),
        in_specs=[ANY],
        out_specs=WHOLE,
        scratch_shapes=[
            pltpu.VMEM((2, n - 1, rows, columns), terms.dtype),
            pltpu.VMEM((2, 2, rows, columns), terms.dtype),
            pltpu.SemaphoreType.DMA((2, 2)),
            pltpu.SemaphoreType.DMA((2, n - 1, 2)),
            pltpu.SemaphoreType.DMA((2, n - 1, 2)),
        ],
        cost_estimate=pl.CostEstimate(
            flops=70_000_000_000, bytes_accessed=2 * terms.size, transcendentals=0
        ),
        compiler_params=pltpu.CompilerParams(
            collective_id=ident, has_side_effects=True, vmem_limit_bytes=60_000_000
        ),
        name="ring_scatter",
    )(terms)


def sum_kernel(n, terms, total, landed, send_sem, recv_sem):
    ahead, behind = ring_neighbours()
    index = lax.axis_index("ctx")
    odd = index % 2
    place = (1 - odd) * (index // 2) + odd * (n - 1 - index // 2)
    greet((ahead, behind))

    def slot(way, back):
        return (place + n - back) % n if way == 0 else (place + back) % n

    made = {}

    def send(source, target, step, way):
        copy = send_to(
            source, target, send_sem.at[way, step], recv_sem.at[way, step], (ahead, behind)[way]
        )
        copy.start()
        made[step, way] = copy

    for way in (0, 1):
        send(terms.at[way, slot(way, 1)], landed.at[way, 0], 0, way)
    for step in range(1, n):
        for way in (0, 1):
            made[step - 1, way].wait_recv()
            own = slot(way, step + 1)
            summed = (
                landed[way, step - 1].astype(jnp.float32) + terms[way, own].astype(jnp.float32)
            ).astype(landed.dtype)
            if step < n - 1:
                landed[way, step - 1] = summed
                send(landed.at[way, step - 1], landed.at[way, step], step, way)
            else:
                total[way, own] = summed
                send(total.at[way, own], total.at[way, own], n - 1, way)
    for step in range(n, 2 * n - 2):
        for way in (0, 1):
            made[step - 1, way].wait_recv()
            have = slot(way, step - n + 1)
            send(total.at[way, have], total.at[way, have], step, way)
    for way in (0, 1):
        made[2 * n - 3, way].wait_recv()
    for key in made:
        made[key].wait_send()


def ring_sum(flat, ident):
    n = lax.axis_size("ctx")
    terms = flat.reshape(2, n, flat.size // (2 * n * 128), 128)
    rows = terms.shape[2]
    total = pl.pallas_call(
        lambda *refs: sum_kernel(n, *refs),
        out_shape=jax.ShapeDtypeStruct(terms.shape, terms.dtype),
        in_specs=[WHOLE],
        out_specs=WHOLE,
        scratch_shapes=[
            pltpu.VMEM((2, n - 1, rows, 128), terms.dtype),
            pltpu.SemaphoreType.DMA((2, 2 * n - 2)),
            pltpu.SemaphoreType.DMA((2, 2 * n - 2)),
        ],
        cost_estimate=pl.CostEstimate(
            flops=60_000_000_000, bytes_accessed=4 * terms.size, transcendentals=0
        ),
        compiler_params=pltpu.CompilerParams(collective_id=ident, has_side_effects=True),
        name="ring_sum",
    )(terms)
    return total.reshape(flat.shape)


def packed_terms(pieces, column):
    n = lax.axis_size("ctx")
    shards = lax.axis_size("fsdp")
    rows = pieces[0].shape[0]
    unit = 2 * n * 16 * 128
    width = sum(piece.shape[1] for piece in pieces) + 1
    step = 128
    while (rows // shards) * step % unit:
        step += 128
    full = -(-width // step) * step
    tail = jnp.pad(column.astype(jnp.bfloat16)[:, None], ((0, 0), (0, full - width)))
    return jnp.concatenate([piece.astype(jnp.bfloat16) for piece in pieces] + [tail], axis=1)


def on_device(
    inputs, cotangent, norm1_gain, qkv_weight, out_weight, norm2_gain, gate_up_weight, down_weight
):
    gains = jnp.pad(jnp.stack([norm1_gain, norm2_gain], axis=1), ((0, 0), (0, 126)))
    first = lax.all_gather(
        jnp.concatenate([qkv_weight, gains], axis=1), "fsdp", axis=0, tiled=True
    )
    w_qkv = first[:, : 3 * D]
    gain_one, gain_two = first[:, 3 * D], first[:, 3 * D + 1]
    w_out, w_gate_up, w_down = (
        lax.all_gather(out_weight, "fsdp", axis=0, tiled=True),
        lax.all_gather(gate_up_weight, "fsdp", axis=0, tiled=True),
        lax.all_gather(down_weight, "fsdp", axis=1, tiled=True),
    )
    local_rows = inputs.shape[1]
    first_row = lax.axis_index("ctx") * local_rows
    positions = (first_row + jnp.arange(local_rows, dtype=jnp.int32)).astype(jnp.float32)
    cosine_table, sine_table = rope_tables(positions)
    tokens = inputs[0].astype(jnp.float32)
    normed, norm_back = jax.vjp(layer_norm, tokens, gain_one.astype(jnp.float32))
    normed_low = normed.astype(jnp.bfloat16)
    projected = jnp.dot(normed_low, w_qkv, preferred_element_type=jnp.float32)
    rotated, rope_back = jax.vjp(
        lambda values: split_rope(values, cosine_table, sine_table), projected
    )
    queries = rotated[0].astype(jnp.bfloat16)
    key_heads = rotated[1].astype(jnp.bfloat16)
    value_heads = rotated[2].astype(jnp.bfloat16)
    key_rows = key_heads.reshape(local_rows, D)
    value_rows = value_heads.reshape(local_rows, D)
    span = lax.axis_size("ctx") * local_rows
    kv_slots = ring_gather(jnp.concatenate([key_rows, value_rows], axis=1)).reshape(span, 2 * D)
    all_keys, all_values = kv_slots[:, :D], kv_slots[:, D:]
    stats_start = (
        jnp.full((HEADS, local_rows), -1e30, jnp.float32),
        jnp.zeros((HEADS, local_rows), jnp.float32),
    )

    def visit(running, block_parts, offset):
        peak_old, total_old = running
        scores = jnp.einsum(
            "qhe,khe->hqk", queries, heads_of(block_parts[0]), preferred_element_type=jnp.float32
        )
        peak_new = jnp.maximum(peak_old, jnp.max(scores, axis=-1))
        total_new = total_old * jnp.exp(peak_old - peak_new) + jnp.sum(
            jnp.exp(scores - peak_new[:, :, None]), axis=-1
        )
        return (peak_new, total_new)

    peak, total = by_blocks(
        (all_keys,), stats_start, visit
    )
    log_total = peak + jnp.log(total)
    head_zeros = jnp.zeros((local_rows, HEADS, HEAD_DIM), jnp.float32)

    def visit(running, block_parts, offset):
        scores = jnp.einsum(
            "qhe,khe->hqk", queries, heads_of(block_parts[0]), preferred_element_type=jnp.float32
        )
        probs_low = jnp.exp(scores - log_total[:, :, None]).astype(jnp.bfloat16)
        return running + jnp.einsum(
            "hqk,khe->qhe", probs_low, heads_of(block_parts[1]), preferred_element_type=jnp.float32
        )

    attended = by_blocks(
        (
            all_keys,
            all_values,
        ),
        head_zeros,
        visit,
    )
    attended_low = attended.reshape(local_rows, D).astype(jnp.bfloat16)
    middle = tokens + jnp.dot(attended_low, w_out, preferred_element_type=jnp.float32)
    normed_two, norm_back_two = jax.vjp(layer_norm, middle, gain_two.astype(jnp.float32))
    normed_two_low = normed_two.astype(jnp.bfloat16)
    gate_up = jnp.dot(normed_two_low, w_gate_up, preferred_element_type=jnp.float32)
    hidden, geglu_back = jax.vjp(geglu, gate_up)
    hidden_low = hidden.astype(jnp.bfloat16)
    output = (middle + jnp.dot(hidden_low, w_down, preferred_element_type=jnp.float32)).astype(
        jnp.bfloat16
    )
    upstream = cotangent[0]
    grad_down = jnp.einsum("lf,ld->df", hidden_low, upstream, preferred_element_type=jnp.float32)
    grad_hidden = jnp.einsum("ld,fd->lf", upstream, w_down, preferred_element_type=jnp.float32)
    grad_gate_up = geglu_back(grad_hidden)[0].astype(jnp.bfloat16)
    grad_w_gate_up = jnp.einsum(
        "ld,lf->df", normed_two_low, grad_gate_up, preferred_element_type=jnp.float32
    )
    grad_normed_two = jnp.einsum(
        "lf,df->ld", grad_gate_up, w_gate_up, preferred_element_type=jnp.float32
    )
    grad_middle_part, grad_gain_two = norm_back_two(grad_normed_two)
    grad_middle = upstream.astype(jnp.float32) + grad_middle_part
    grad_branch = grad_middle.astype(jnp.bfloat16)
    grad_w_out = jnp.einsum(
        "ld,le->de", attended_low, grad_branch, preferred_element_type=jnp.float32
    )
    grad_attended = jnp.einsum(
        "le,de->ld", grad_branch, w_out, preferred_element_type=jnp.float32
    ).astype(jnp.bfloat16)
    grad_heads = heads_of(grad_attended)
    delta_rows = jnp.sum(grad_heads.astype(jnp.float32) * attended, axis=-1).T
    back_start = (head_zeros, jnp.zeros((2, span, D), jnp.bfloat16))

    def visit(running, block_parts, offset):
        grad_query, grad_kv = running
        key_block = heads_of(block_parts[0])
        value_block = heads_of(block_parts[1])
        probs_low, grad_scores = score_parts(
            queries, key_block, value_block, grad_heads, log_total, delta_rows
        )
        grad_query = grad_query + jnp.einsum(
            "hqk,khe->qhe", grad_scores, key_block, preferred_element_type=jnp.float32
        )
        grad_key = jnp.einsum(
            "hqk,qhe->khe", grad_scores, queries, preferred_element_type=jnp.float32
        )
        grad_value = jnp.einsum(
            "hqk,qhe->khe", probs_low, grad_heads, preferred_element_type=jnp.float32
        )
        update = jnp.stack([grad_key.reshape(-1, D), grad_value.reshape(-1, D)], axis=0)
        grad_kv = lax.dynamic_update_slice(grad_kv, update.astype(jnp.bfloat16), (0, offset, 0))
        return (grad_query, grad_kv)

    grad_query, grad_kv_all = by_blocks(
        (
            all_keys,
            all_values,
        ),
        back_start,
        visit,
    )
    grad_kv = ring_scatter(
        grad_kv_all.reshape(2, -1, local_rows, D), jnp.bfloat16, 2
    ).astype(jnp.float32)
    grad_key_sum = heads_of(grad_kv[0])
    grad_value_sum = heads_of(grad_kv[1])
    grad_rotated = (rounded(grad_query), grad_key_sum, grad_value_sum)
    grad_projected = rope_back(grad_rotated)[0].astype(jnp.bfloat16)
    grad_w_qkv = jnp.einsum(
        "ld,lf->df", normed_low, grad_projected, preferred_element_type=jnp.float32
    )
    grad_normed = jnp.einsum("lf,df->ld", grad_projected, w_qkv, preferred_element_type=jnp.float32)
    grad_tokens_part, grad_gain_one = norm_back(grad_normed)
    input_grad = grad_middle + grad_tokens_part
    shard_one = lax.psum_scatter(
        packed_terms((grad_w_gate_up, grad_down, grad_w_out), grad_gain_two),
        "fsdp",
        scatter_dimension=0,
        tiled=True,
    )
    shard_two = lax.psum_scatter(
        packed_terms((grad_w_qkv,), grad_gain_one), "fsdp", scatter_dimension=0, tiled=True
    )
    total_one = ring_sum(shard_one, 3).astype(jnp.float32)
    total_two = ring_sum(shard_two, 4).astype(jnp.float32)
    up_end, down_end, out_end = 2 * FF, 3 * FF, 3 * FF + D
    return (
        output[None],
        input_grad[None],
        total_two[:, 3 * D],
        total_one[:, out_end],
        total_two[:, : 3 * D],
        total_one[:, down_end:out_end],
        total_one[:, :up_end],
        total_one[:, up_end:down_end].T,
    )


def solution(mesh):
    in_specs = (
        P("fsdp", "ctx", None),
        P("fsdp", "ctx", None),
        P("fsdp"),
        P("fsdp", None),
        P("fsdp", None),
        P("fsdp"),
        P("fsdp", None),
        P(None, "fsdp"),
    )
    out_specs = (
        P("fsdp", "ctx", None),
        P("fsdp", "ctx", None),
        P("fsdp"),
        P("fsdp"),
        P("fsdp", None),
        P("fsdp", None),
        P("fsdp", None),
        P(None, "fsdp"),
    )
    return jax.shard_map(
        on_device, mesh=mesh, in_specs=in_specs, out_specs=out_specs, check_vma=False
    )
```

```python
import math

import jax
import jax.numpy as jnp
from jax import lax
from jax.experimental import pallas as pl
from jax.experimental.pallas import tpu as pltpu
from jax.sharding import PartitionSpec as P

D = 768
HEADS = 12
HEAD_DIM = 64
FF = 1152


def layer_norm(values, norm_gain):
    center = values - jnp.mean(values, axis=-1, keepdims=True)
    spread = jnp.mean(center * center, axis=-1, keepdims=True)
    return center * lax.rsqrt(spread + 1e-05) * norm_gain


def rotate(values, cosine_table, sine_table):
    half_size = values.shape[-1] // 2
    leading = values[..., :half_size]
    trailing = values[..., half_size:]
    return jnp.concatenate(
        [
            leading * cosine_table - trailing * sine_table,
            trailing * cosine_table + leading * sine_table,
        ],
        axis=-1,
    )


def rope_tables(positions):
    indices = jnp.arange(HEAD_DIM // 2).astype(jnp.float32)
    frequency = jnp.exp(indices * (-2.0 * math.log(160000.0) / HEAD_DIM))
    angles = positions[:, None] * frequency[None, :]
    return (jnp.cos(angles)[:, None, :], jnp.sin(angles)[:, None, :])


def gelu_exact(values):
    return 0.5 * values * (1.0 + jax.scipy.special.erf(values * 0.7071067811865476))


def geglu(gate_up):
    return gelu_exact(gate_up[:, :FF]) * gate_up[:, FF:]


def split_rope(projected, cosine_table, sine_table):
    heads_view = projected.reshape(projected.shape[0], 3, HEADS, HEAD_DIM)
    return (
        rotate(heads_view[:, 0], cosine_table, sine_table) * 0.125,
        rotate(heads_view[:, 1], cosine_table, sine_table),
        heads_view[:, 2],
    )


def heads_of(flat_rows):
    return flat_rows.reshape(flat_rows.shape[0], HEADS, HEAD_DIM)


def rounded(values):
    return lax.optimization_barrier(values.astype(jnp.bfloat16)).astype(jnp.float32)


MESH = pl.DeviceIdType.MESH
ANY = pl.BlockSpec(memory_space=pl.ANY)
WHOLE = pl.BlockSpec(memory_space=pltpu.VMEM)


def ring_neighbours():
    n = lax.axis_size("ctx")
    index = lax.axis_index("ctx")
    odd = index % 2
    place = (1 - odd) * (index // 2) + odd * (n - 1 - index // 2)

    def index_of(position):
        upper = position // (n // 2)
        return (1 - upper) * 2 * position + upper * (2 * (n - 1 - position) + 1)

    return index_of((place + 1) % n), index_of((place + n - 1) % n)


def send_to(source, target, send_sem, recv_sem, index):
    return pltpu.make_async_remote_copy(
        src_ref=source,
        dst_ref=target,
        send_sem=send_sem,
        recv_sem=recv_sem,
        device_id={"ctx": index},
        device_id_type=MESH,
    )


def greet(neighbours):
    barrier = pltpu.get_barrier_semaphore()
    for index in neighbours:
        pl.semaphore_signal(barrier, inc=1, device_id={"ctx": index}, device_id_type=MESH)
    pl.semaphore_wait(barrier, 2)


def half_of(values, half):
    lane = lax.broadcasted_iota(jnp.int32, values.shape, 1)
    keep = lane < HEAD_DIM if half == 0 else lane >= HEAD_DIM
    return jnp.where(keep, values, jnp.zeros_like(values))


def times_t(left, right):
    return lax.dot_general(
        left, right, (((1,), (1,)), ((), ())), preferred_element_type=jnp.float32
    )


def times(left, right):
    return jnp.dot(left, right, preferred_element_type=jnp.float32)


def attend_kernel(
    n, own, queries, slots, attended, logs, held, peak, total, gathered, local_sem, send_sem, recv_sem
):
    ahead, behind = ring_neighbours()
    half = own.shape[0] // 2
    greet((ahead, behind))
    keep = pltpu.make_async_copy(own, slots.at[0], local_sem.at[2])
    keep.start()
    parts = (pl.ds(0, half), pl.ds(half, half))
    steps = n // 2
    made = {}

    def send(step, way, part):
        here, there = (step, step + 1) if way == 0 else ((n - step) % n, n - step - 1)
        source = own if step == 0 else slots.at[here]
        copy = send_to(
            source.at[parts[part]],
            slots.at[there, parts[part]],
            send_sem.at[way, step, part],
            recv_sem.at[way, step, part],
            (ahead, behind)[way],
        )
        copy.start()
        made[step, way, part] = copy

    def attend(block):
        def pair(h, carry):
            at = pl.multiple_of((h // 3) * D + (h % 3) * 128, 128)
            keys = block[:, pl.ds(at, 128)]
            values_t = block[:, pl.ds(pl.multiple_of(at + D // 2, 128), 128)].T
            rows = queries[:, pl.ds(pl.multiple_of(h * 128, 128), 128)]
            for side in (0, 1):
                scores = times_t(keys, half_of(rows, side))
                old = peak[2 * h + side]
                new = jnp.maximum(old, jnp.max(scores, axis=0, keepdims=True))
                weights = jnp.exp(scores - new)
                scale = jnp.exp(old - new)
                peak[2 * h + side] = new
                total[2 * h + side] = total[2 * h + side] * scale + jnp.sum(
                    weights, axis=0, keepdims=True
                )
                lanes = pl.ds(side * HEAD_DIM, HEAD_DIM)
                gathered[h, lanes] = gathered[h, lanes] * scale + times(
                    values_t[side * HEAD_DIM : (side + 1) * HEAD_DIM], weights.astype(jnp.bfloat16)
                )
            return carry

        lax.fori_loop(0, HEADS // 2, pair, 0)

    for way in (0, 1):
        for part in (0, 1):
            if steps > 1 or part == way:
                send(0, way, part)
    peak[...] = jnp.full(peak.shape, -1e30, jnp.float32)
    total[...] = jnp.zeros(total.shape, jnp.float32)
    gathered[...] = jnp.zeros(gathered.shape, jnp.float32)
    attend(own)
    for step in range(1, steps):
        for part in (0, 1):
            for way in (0, 1):
                made[step - 1, way, part].wait_recv()
                if step < steps - 1 or part == way:
                    send(step, way, part)
        loads = [
            pltpu.make_async_copy(
                slots.at[step if way == 0 else n - step], held.at[way], local_sem.at[way]
            )
            for way in (0, 1)
        ]
        for load in loads:
            load.start()
        for way in (0, 1):
            loads[way].wait()
            attend(held.at[way])
    for way in (0, 1):
        made[steps - 1, way, way].wait_recv()
    load = pltpu.make_async_copy(slots.at[steps], held.at[0], local_sem.at[0])
    load.start()
    load.wait()
    attend(held.at[0])
    for h in range(HEADS // 2):
        for side in (0, 1):
            lanes = pl.ds(side * HEAD_DIM, HEAD_DIM)
            gathered[h, lanes] = gathered[h, lanes] / total[2 * h + side]
        attended[:, h * 128 : (h + 1) * 128] = gathered[h].T
    logs[...] = peak[...] + jnp.log(total[...])
    for key in made:
        made[key].wait_send()
    keep.wait()


def ring_attend(block, queries):
    n = lax.axis_size("ctx")
    rows, columns = block.shape
    return pl.pallas_call(
        lambda *refs: attend_kernel(n, *refs),
        out_shape=(
            jax.ShapeDtypeStruct((n, rows, columns), block.dtype),
            jax.ShapeDtypeStruct((rows, D), jnp.float32),
            jax.ShapeDtypeStruct((HEADS, 1, rows), jnp.float32),
        ),
        in_specs=[WHOLE, WHOLE],
        out_specs=(ANY, WHOLE, WHOLE),
        scratch_shapes=[
            pltpu.VMEM((2, rows, columns), block.dtype),
            pltpu.VMEM((HEADS, 1, rows), jnp.float32),
            pltpu.VMEM((HEADS, 1, rows), jnp.float32),
            pltpu.VMEM((HEADS // 2, 128, rows), jnp.float32),
            pltpu.SemaphoreType.DMA((3,)),
            pltpu.SemaphoreType.DMA((2, n // 2, 2)),
            pltpu.SemaphoreType.DMA((2, n // 2, 2)),
        ],
        cost_estimate=pl.CostEstimate(
            flops=70_000_000_000, bytes_accessed=2 * n * block.size, transcendentals=0
        ),
        compiler_params=pltpu.CompilerParams(
            collective_id=1, has_side_effects=True, vmem_limit_bytes=60_000_000
        ),
        name="ring_attend",
    )(block, queries)


def back_kernel(
    n, queries, grads, logs, deltas, slots, total, grad_queries,
    landed, first, fresh, held, load_sem, send_sem, recv_sem,
):
    ahead, behind = ring_neighbours()
    half = total.shape[1] // 2
    parts = (pl.ds(0, half), pl.ds(half, half))

    def load(step, way):
        slot = (step + 1) % n if way == 0 else (2 * n - step - 1) % n
        return pltpu.make_async_copy(
            slots.at[slot, :, pl.ds(way * D, D)], held.at[way], load_sem.at[way]
        )

    def terms(way, target):
        def pair(r, carry):
            h = 3 * way + r
            at = pl.multiple_of(r * 128, 128)
            after = pl.multiple_of(r * 128 + D // 2, 128)
            here = pl.ds(pl.multiple_of(h * 128, 128), 128)
            keys = held[way, :, pl.ds(at, 128)]
            values = held[way, :, pl.ds(after, 128)]
            keys_t = keys.T
            grad_key, grad_value = 0.0, 0.0
            for side in (0, 1):
                rows = half_of(queries[:, here], side)
                grad_rows = half_of(grads[:, here], side)
                probs = jnp.exp(times_t(keys, rows) - logs[2 * h + side])
                grad_probs = times_t(values, grad_rows)
                grad_scores = (probs * (grad_probs - deltas[2 * h + side])).astype(jnp.bfloat16)
                grad_value += times(probs.astype(jnp.bfloat16), grad_rows)
                grad_key += times(grad_scores, rows)
                lanes = pl.ds(side * HEAD_DIM, HEAD_DIM)
                grad_queries[h, lanes] += times(
                    keys_t[side * HEAD_DIM : (side + 1) * HEAD_DIM], grad_scores
                )
            target[way, :, pl.ds(at, 128)] = grad_key.astype(target.dtype)
            target[way, :, pl.ds(after, 128)] = grad_value.astype(target.dtype)
            return carry

        lax.fori_loop(0, HEADS // 4, pair, 0)

    for way in (0, 1):
        load(0, way).start()
    grad_queries[...] = jnp.zeros(grad_queries.shape, jnp.float32)
    greet((ahead, behind))
    made = {}

    def send(step, way, part):
        source = first.at[way] if step == 0 else landed.at[way, step - 1]
        copy = send_to(
            source.at[parts[part]],
            landed.at[way, step, parts[part]],
            send_sem.at[way, step, part],
            recv_sem.at[way, step, part],
            (ahead, behind)[way],
        )
        copy.start()
        made[step, way, part] = copy

    for way in (0, 1):
        load(0, way).wait()
        terms(way, first)
        for part in (0, 1):
            send(0, way, part)
        load(1, way).start()
    for step in range(1, n):
        for way in (0, 1):
            load(step, way).wait()
            terms(way, fresh)
            if step + 1 < n:
                load(step + 1, way).start()
        for part in (0, 1):
            for way in (0, 1):
                made[step - 1, way, part].wait_recv()
                rows = parts[part]
                summed = landed[way, step - 1, rows].astype(jnp.float32) + fresh[way, rows].astype(
                    jnp.float32
                )
                if step == n - 1:
                    total[way, rows] = summed.astype(total.dtype)
                else:
                    landed[way, step - 1, rows] = summed.astype(landed.dtype)
                    send(step, way, part)
    for key in made:
        made[key].wait_send()


def ring_back(queries, grads, logs, deltas, slots):
    n, rows, _ = slots.shape
    return pl.pallas_call(
        lambda *refs: back_kernel(n, *refs),
        out_shape=(
            jax.ShapeDtypeStruct((2, rows, D), jnp.bfloat16),
            jax.ShapeDtypeStruct((HEADS // 2, 128, rows), jnp.float32),
        ),
        in_specs=[WHOLE, WHOLE, WHOLE, WHOLE, ANY],
        out_specs=(WHOLE, WHOLE),
        scratch_shapes=[
            pltpu.VMEM((2, n - 1, rows, D), jnp.bfloat16),
            pltpu.VMEM((2, rows, D), jnp.bfloat16),
            pltpu.VMEM((2, rows, D), jnp.bfloat16),
            pltpu.VMEM((2, rows, D), jnp.bfloat16),
            pltpu.SemaphoreType.DMA((2,)),
            pltpu.SemaphoreType.DMA((2, n - 1, 2)),
            pltpu.SemaphoreType.DMA((2, n - 1, 2)),
        ],
        cost_estimate=pl.CostEstimate(
            flops=80_000_000_000, bytes_accessed=2 * slots.size, transcendentals=0
        ),
        compiler_params=pltpu.CompilerParams(
            collective_id=2, has_side_effects=True, vmem_limit_bytes=67_000_000
        ),
        name="ring_back",
    )(queries, grads, logs, deltas, slots)


def sum_kernel(n, terms, total, landed, send_sem, recv_sem):
    ahead, behind = ring_neighbours()
    index = lax.axis_index("ctx")
    odd = index % 2
    place = (1 - odd) * (index // 2) + odd * (n - 1 - index // 2)
    greet((ahead, behind))

    def slot(way, back):
        return (place + n - back) % n if way == 0 else (place + back) % n

    made = {}

    def send(source, target, step, way):
        copy = send_to(
            source, target, send_sem.at[way, step], recv_sem.at[way, step], (ahead, behind)[way]
        )
        copy.start()
        made[step, way] = copy

    for way in (0, 1):
        send(terms.at[way, slot(way, 1)], landed.at[way, 0], 0, way)
    for step in range(1, n):
        for way in (0, 1):
            made[step - 1, way].wait_recv()
            own = slot(way, step + 1)
            summed = (
                landed[way, step - 1].astype(jnp.float32) + terms[way, own].astype(jnp.float32)
            ).astype(landed.dtype)
            if step < n - 1:
                landed[way, step - 1] = summed
                send(landed.at[way, step - 1], landed.at[way, step], step, way)
            else:
                total[way, own] = summed
                send(total.at[way, own], total.at[way, own], n - 1, way)
    for step in range(n, 2 * n - 2):
        for way in (0, 1):
            made[step - 1, way].wait_recv()
            have = slot(way, step - n + 1)
            send(total.at[way, have], total.at[way, have], step, way)
    for way in (0, 1):
        made[2 * n - 3, way].wait_recv()
    for key in made:
        made[key].wait_send()


def ring_sum(flat, ident):
    n = lax.axis_size("ctx")
    terms = flat.reshape(2, n, flat.size // (2 * n * 128), 128)
    rows = terms.shape[2]
    total = pl.pallas_call(
        lambda *refs: sum_kernel(n, *refs),
        out_shape=jax.ShapeDtypeStruct(terms.shape, terms.dtype),
        in_specs=[WHOLE],
        out_specs=WHOLE,
        scratch_shapes=[
            pltpu.VMEM((2, n - 1, rows, 128), terms.dtype),
            pltpu.SemaphoreType.DMA((2, 2 * n - 2)),
            pltpu.SemaphoreType.DMA((2, 2 * n - 2)),
        ],
        cost_estimate=pl.CostEstimate(
            flops=60_000_000_000, bytes_accessed=4 * terms.size, transcendentals=0
        ),
        compiler_params=pltpu.CompilerParams(collective_id=ident, has_side_effects=True),
        name="ring_sum",
    )(terms)
    return total.reshape(flat.shape)


def packed_terms(pieces, column):
    n = lax.axis_size("ctx")
    shards = lax.axis_size("fsdp")
    rows = pieces[0].shape[0]
    unit = 2 * n * 16 * 128
    width = sum(piece.shape[1] for piece in pieces) + 1
    step = 128
    while (rows // shards) * step % unit:
        step += 128
    full = -(-width // step) * step
    tail = jnp.pad(column.astype(jnp.bfloat16)[:, None], ((0, 0), (0, full - width)))
    return jnp.concatenate([piece.astype(jnp.bfloat16) for piece in pieces] + [tail], axis=1)


def on_device(
    inputs, cotangent, norm1_gain, qkv_weight, out_weight, norm2_gain, gate_up_weight, down_weight
):
    gains = jnp.pad(jnp.stack([norm1_gain, norm2_gain], axis=1), ((0, 0), (0, 126)))
    first = lax.all_gather(
        jnp.concatenate([qkv_weight, gains], axis=1), "fsdp", axis=0, tiled=True
    )
    w_qkv = first[:, : 3 * D]
    gain_one, gain_two = first[:, 3 * D], first[:, 3 * D + 1]
    w_out, w_gate_up, w_down = (
        lax.all_gather(out_weight, "fsdp", axis=0, tiled=True),
        lax.all_gather(gate_up_weight, "fsdp", axis=0, tiled=True),
        lax.all_gather(down_weight, "fsdp", axis=1, tiled=True),
    )
    local_rows = inputs.shape[1]
    first_row = lax.axis_index("ctx") * local_rows
    positions = (first_row + jnp.arange(local_rows, dtype=jnp.int32)).astype(jnp.float32)
    cosine_table, sine_table = rope_tables(positions)
    tokens = inputs[0].astype(jnp.float32)
    normed, norm_back = jax.vjp(layer_norm, tokens, gain_one.astype(jnp.float32))
    normed_low = normed.astype(jnp.bfloat16)
    projected = jnp.dot(normed_low, w_qkv, preferred_element_type=jnp.float32)
    rotated, rope_back = jax.vjp(
        lambda values: split_rope(values, cosine_table, sine_table), projected
    )
    queries = rotated[0].astype(jnp.bfloat16).reshape(local_rows, D)
    key_rows = rotated[1].astype(jnp.bfloat16).reshape(local_rows, D)
    value_rows = rotated[2].astype(jnp.bfloat16).reshape(local_rows, D)
    cut = D // 2
    block = jnp.concatenate(
        [key_rows[:, :cut], value_rows[:, :cut], key_rows[:, cut:], value_rows[:, cut:]], axis=1
    )
    slots, attended, log_total = ring_attend(block, queries)
    attended_low = attended.astype(jnp.bfloat16)
    middle = tokens + jnp.dot(attended_low, w_out, preferred_element_type=jnp.float32)
    normed_two, norm_back_two = jax.vjp(layer_norm, middle, gain_two.astype(jnp.float32))
    normed_two_low = normed_two.astype(jnp.bfloat16)
    gate_up = jnp.dot(normed_two_low, w_gate_up, preferred_element_type=jnp.float32)
    hidden, geglu_back = jax.vjp(geglu, gate_up)
    hidden_low = hidden.astype(jnp.bfloat16)
    output = (middle + jnp.dot(hidden_low, w_down, preferred_element_type=jnp.float32)).astype(
        jnp.bfloat16
    )
    upstream = cotangent[0]
    grad_down = jnp.einsum("lf,ld->df", hidden_low, upstream, preferred_element_type=jnp.float32)
    grad_hidden = jnp.einsum("ld,fd->lf", upstream, w_down, preferred_element_type=jnp.float32)
    grad_gate_up = geglu_back(grad_hidden)[0].astype(jnp.bfloat16)
    grad_w_gate_up = jnp.einsum(
        "ld,lf->df", normed_two_low, grad_gate_up, preferred_element_type=jnp.float32
    )
    grad_normed_two = jnp.einsum(
        "lf,df->ld", grad_gate_up, w_gate_up, preferred_element_type=jnp.float32
    )
    grad_middle_part, grad_gain_two = norm_back_two(grad_normed_two)
    grad_middle = upstream.astype(jnp.float32) + grad_middle_part
    grad_branch = grad_middle.astype(jnp.bfloat16)
    grad_w_out = jnp.einsum(
        "ld,le->de", attended_low, grad_branch, preferred_element_type=jnp.float32
    )
    grad_attended = jnp.einsum(
        "le,de->ld", grad_branch, w_out, preferred_element_type=jnp.float32
    ).astype(jnp.bfloat16)
    deltas = jnp.sum(
        heads_of(grad_attended.astype(jnp.float32) * attended), axis=-1
    ).T[:, None, :]
    packed_one = packed_terms((grad_w_gate_up, grad_down, grad_w_out), grad_gain_two)
    packed_one, grad_attended, deltas = lax.optimization_barrier(
        (packed_one, grad_attended, deltas)
    )
    shard_one = lax.psum_scatter(packed_one, "fsdp", scatter_dimension=0, tiled=True)
    grad_kv, grad_query_t = ring_back(queries, grad_attended, log_total, deltas, slots)
    grad_query = grad_query_t.reshape(D, local_rows).T
    grad_key = jnp.concatenate([grad_kv[0, :, :cut], grad_kv[1, :, :cut]], axis=1)
    grad_value = jnp.concatenate([grad_kv[0, :, cut:], grad_kv[1, :, cut:]], axis=1)
    grad_rotated = (
        rounded(heads_of(grad_query)),
        heads_of(grad_key.astype(jnp.float32)),
        heads_of(grad_value.astype(jnp.float32)),
    )
    grad_projected = rope_back(grad_rotated)[0].astype(jnp.bfloat16)
    grad_w_qkv = jnp.einsum(
        "ld,lf->df", normed_low, grad_projected, preferred_element_type=jnp.float32
    )
    grad_normed = jnp.einsum("lf,df->ld", grad_projected, w_qkv, preferred_element_type=jnp.float32)
    grad_tokens_part, grad_gain_one = norm_back(grad_normed)
    input_grad = grad_middle + grad_tokens_part
    shard_two = lax.psum_scatter(
        packed_terms((grad_w_qkv,), grad_gain_one), "fsdp", scatter_dimension=0, tiled=True
    )
    total_one = ring_sum(shard_one, 3).astype(jnp.float32)
    total_two = ring_sum(shard_two, 4).astype(jnp.float32)
    up_end, down_end, out_end = 2 * FF, 3 * FF, 3 * FF + D
    return (
        output[None],
        input_grad[None],
        total_two[:, 3 * D],
        total_one[:, out_end],
        total_two[:, : 3 * D],
        total_one[:, down_end:out_end],
        total_one[:, :up_end],
        total_one[:, up_end:down_end].T,
    )


def solution(mesh):
    in_specs = (
        P("fsdp", "ctx", None),
        P("fsdp", "ctx", None),
        P("fsdp"),
        P("fsdp", None),
        P("fsdp", None),
        P("fsdp"),
        P("fsdp", None),
        P(None, "fsdp"),
    )
    out_specs = (
        P("fsdp", "ctx", None),
        P("fsdp", "ctx", None),
        P("fsdp"),
        P("fsdp"),
        P("fsdp", None),
        P("fsdp", None),
        P("fsdp", None),
        P(None, "fsdp"),
    )
    return jax.shard_map(
        on_device, mesh=mesh, in_specs=in_specs, out_specs=out_specs, check_vma=False
    )
```

```python
import math

import jax
import jax.numpy as jnp
from jax import lax
from jax.experimental import pallas as pl
from jax.experimental.pallas import tpu as pltpu
from jax.sharding import PartitionSpec as P

D = 768
HEADS = 12
HEAD_DIM = 64
FF = 1152


def layer_norm(values, norm_gain):
    center = values - jnp.mean(values, axis=-1, keepdims=True)
    spread = jnp.mean(center * center, axis=-1, keepdims=True)
    return center * lax.rsqrt(spread + 1e-05) * norm_gain


def rotate(values, cosine_table, sine_table):
    half_size = values.shape[-1] // 2
    leading = values[..., :half_size]
    trailing = values[..., half_size:]
    return jnp.concatenate(
        [
            leading * cosine_table - trailing * sine_table,
            trailing * cosine_table + leading * sine_table,
        ],
        axis=-1,
    )


def rope_tables(positions):
    indices = jnp.arange(HEAD_DIM // 2).astype(jnp.float32)
    frequency = jnp.exp(indices * (-2.0 * math.log(160000.0) / HEAD_DIM))
    angles = positions[:, None] * frequency[None, :]
    return (jnp.cos(angles)[:, None, :], jnp.sin(angles)[:, None, :])


def gelu_exact(values):
    return 0.5 * values * (1.0 + jax.scipy.special.erf(values * 0.7071067811865476))


def geglu(gate_up):
    return gelu_exact(gate_up[:, :FF]) * gate_up[:, FF:]


def split_rope(projected, cosine_table, sine_table):
    heads_view = projected.reshape(projected.shape[0], 3, HEADS, HEAD_DIM)
    return (
        rotate(heads_view[:, 0], cosine_table, sine_table) * 0.125,
        rotate(heads_view[:, 1], cosine_table, sine_table),
        heads_view[:, 2],
    )


def heads_of(flat_rows):
    return flat_rows.reshape(flat_rows.shape[0], HEADS, HEAD_DIM)


def rounded(values):
    return lax.optimization_barrier(values.astype(jnp.bfloat16)).astype(jnp.float32)


MESH = pl.DeviceIdType.MESH
ANY = pl.BlockSpec(memory_space=pl.ANY)
WHOLE = pl.BlockSpec(memory_space=pltpu.VMEM)


def ring_neighbours():
    n = lax.axis_size("ctx")
    index = lax.axis_index("ctx")
    odd = index % 2
    place = (1 - odd) * (index // 2) + odd * (n - 1 - index // 2)

    def index_of(position):
        upper = position // (n // 2)
        return (1 - upper) * 2 * position + upper * (2 * (n - 1 - position) + 1)

    return index_of((place + 1) % n), index_of((place + n - 1) % n)


def send_to(source, target, send_sem, recv_sem, index):
    return pltpu.make_async_remote_copy(
        src_ref=source,
        dst_ref=target,
        send_sem=send_sem,
        recv_sem=recv_sem,
        device_id={"ctx": index},
        device_id_type=MESH,
    )


def greet(neighbours):
    barrier = pltpu.get_barrier_semaphore()
    for index in neighbours:
        pl.semaphore_signal(barrier, inc=1, device_id={"ctx": index}, device_id_type=MESH)
    pl.semaphore_wait(barrier, 2)


def half_of(values, half):
    lane = lax.broadcasted_iota(jnp.int32, values.shape, 1)
    keep = lane < HEAD_DIM if half == 0 else lane >= HEAD_DIM
    return jnp.where(keep, values, jnp.zeros_like(values))


def times_t(left, right):
    return lax.dot_general(
        left, right, (((1,), (1,)), ((), ())), preferred_element_type=jnp.float32
    )


def times(left, right):
    return jnp.dot(left, right, preferred_element_type=jnp.float32)


def attend_kernel(
    n, own, queries, slots, attended, logs, held, peak, total, gathered, local_sem, send_sem, recv_sem
):
    ahead, behind = ring_neighbours()
    half = own.shape[0] // 2
    greet((ahead, behind))
    keep = pltpu.make_async_copy(own, slots.at[0], local_sem.at[2])
    keep.start()
    parts = (pl.ds(0, half), pl.ds(half, half))
    steps = n // 2
    made = {}

    def send(step, way, part):
        here, there = (step, step + 1) if way == 0 else ((n - step) % n, n - step - 1)
        source = own if step == 0 else slots.at[here]
        copy = send_to(
            source.at[parts[part]],
            slots.at[there, parts[part]],
            send_sem.at[way, step, part],
            recv_sem.at[way, step, part],
            (ahead, behind)[way],
        )
        copy.start()
        made[step, way, part] = copy

    def attend(block):
        def pair(h, carry):
            at = pl.multiple_of((h // 3) * D + (h % 3) * 128, 128)
            keys = block[:, pl.ds(at, 128)]
            values_t = block[:, pl.ds(pl.multiple_of(at + D // 2, 128), 128)].T
            rows = queries[:, pl.ds(pl.multiple_of(h * 128, 128), 128)]
            for side in (0, 1):
                scores = times_t(keys, half_of(rows, side))
                old = peak[2 * h + side]
                new = jnp.maximum(old, jnp.max(scores, axis=0, keepdims=True))
                weights = jnp.exp(scores - new)
                scale = jnp.exp(old - new)
                peak[2 * h + side] = new
                total[2 * h + side] = total[2 * h + side] * scale + jnp.sum(
                    weights, axis=0, keepdims=True
                )
                lanes = pl.ds(side * HEAD_DIM, HEAD_DIM)
                gathered[h, lanes] = gathered[h, lanes] * scale + times(
                    values_t[side * HEAD_DIM : (side + 1) * HEAD_DIM], weights.astype(jnp.bfloat16)
                )
            return carry

        lax.fori_loop(0, HEADS // 2, pair, 0)

    for way in (0, 1):
        for part in (0, 1):
            if steps > 1 or part == way:
                send(0, way, part)
    peak[...] = jnp.full(peak.shape, -1e30, jnp.float32)
    total[...] = jnp.zeros(total.shape, jnp.float32)
    gathered[...] = jnp.zeros(gathered.shape, jnp.float32)
    attend(own)
    for step in range(1, steps):
        for part in (0, 1):
            for way in (0, 1):
                made[step - 1, way, part].wait_recv()
                if step < steps - 1 or part == way:
                    send(step, way, part)
        loads = [
            pltpu.make_async_copy(
                slots.at[step if way == 0 else n - step], held.at[way], local_sem.at[way]
            )
            for way in (0, 1)
        ]
        for load in loads:
            load.start()
        for way in (0, 1):
            loads[way].wait()
            attend(held.at[way])
    for way in (0, 1):
        made[steps - 1, way, way].wait_recv()
    load = pltpu.make_async_copy(slots.at[steps], held.at[0], local_sem.at[0])
    load.start()
    load.wait()
    attend(held.at[0])
    for h in range(HEADS // 2):
        for side in (0, 1):
            lanes = pl.ds(side * HEAD_DIM, HEAD_DIM)
            gathered[h, lanes] = gathered[h, lanes] / total[2 * h + side]
        attended[:, h * 128 : (h + 1) * 128] = gathered[h].T
    logs[...] = peak[...] + jnp.log(total[...])
    for key in made:
        made[key].wait_send()
    keep.wait()


def ring_attend(block, queries):
    n = lax.axis_size("ctx")
    rows, columns = block.shape
    return pl.pallas_call(
        lambda *refs: attend_kernel(n, *refs),
        out_shape=(
            jax.ShapeDtypeStruct((n, rows, columns), block.dtype),
            jax.ShapeDtypeStruct((rows, D), jnp.float32),
            jax.ShapeDtypeStruct((HEADS, 1, rows), jnp.float32),
        ),
        in_specs=[WHOLE, WHOLE],
        out_specs=(ANY, WHOLE, WHOLE),
        scratch_shapes=[
            pltpu.VMEM((2, rows, columns), block.dtype),
            pltpu.VMEM((HEADS, 1, rows), jnp.float32),
            pltpu.VMEM((HEADS, 1, rows), jnp.float32),
            pltpu.VMEM((HEADS // 2, 128, rows), jnp.float32),
            pltpu.SemaphoreType.DMA((3,)),
            pltpu.SemaphoreType.DMA((2, n // 2, 2)),
            pltpu.SemaphoreType.DMA((2, n // 2, 2)),
        ],
        cost_estimate=pl.CostEstimate(
            flops=70_000_000_000, bytes_accessed=2 * n * block.size, transcendentals=0
        ),
        compiler_params=pltpu.CompilerParams(
            collective_id=1, has_side_effects=True, vmem_limit_bytes=60_000_000
        ),
        name="ring_attend",
    )(block, queries)


def back_kernel(
    n, queries, grads, logs, deltas, slots, total, grad_queries,
    landed, first, fresh, held, load_sem, send_sem, recv_sem,
):
    ahead, behind = ring_neighbours()
    half = total.shape[1] // 2
    parts = (pl.ds(0, half), pl.ds(half, half))

    def load(step, way):
        slot = (step + 1) % n if way == 0 else (2 * n - step - 1) % n
        return pltpu.make_async_copy(
            slots.at[slot, :, pl.ds(way * D, D)], held.at[way], load_sem.at[way]
        )

    def terms(way, target):
        def pair(r, carry):
            h = 3 * way + r
            at = pl.multiple_of(r * 128, 128)
            after = pl.multiple_of(r * 128 + D // 2, 128)
            here = pl.ds(pl.multiple_of(h * 128, 128), 128)
            keys = held[way, :, pl.ds(at, 128)]
            values = held[way, :, pl.ds(after, 128)]
            keys_t = keys.T
            grad_key, grad_value = 0.0, 0.0
            for side in (0, 1):
                rows = half_of(queries[:, here], side)
                grad_rows = half_of(grads[:, here], side)
                probs = jnp.exp(times_t(keys, rows) - logs[2 * h + side])
                grad_probs = times_t(values, grad_rows)
                grad_scores = (probs * (grad_probs - deltas[2 * h + side])).astype(jnp.bfloat16)
                grad_value += times(probs.astype(jnp.bfloat16), grad_rows)
                grad_key += times(grad_scores, rows)
                lanes = pl.ds(side * HEAD_DIM, HEAD_DIM)
                grad_queries[h, lanes] += times(
                    keys_t[side * HEAD_DIM : (side + 1) * HEAD_DIM], grad_scores
                )
            target[way, :, pl.ds(at, 128)] = grad_key.astype(target.dtype)
            target[way, :, pl.ds(after, 128)] = grad_value.astype(target.dtype)
            return carry

        lax.fori_loop(0, HEADS // 4, pair, 0)

    for way in (0, 1):
        load(0, way).start()
    grad_queries[...] = jnp.zeros(grad_queries.shape, jnp.float32)
    greet((ahead, behind))
    made = {}

    def send(step, way, part):
        source = first.at[way] if step == 0 else landed.at[way, step - 1]
        copy = send_to(
            source.at[parts[part]],
            landed.at[way, step, parts[part]],
            send_sem.at[way, step, part],
            recv_sem.at[way, step, part],
            (ahead, behind)[way],
        )
        copy.start()
        made[step, way, part] = copy

    for way in (0, 1):
        load(0, way).wait()
        terms(way, first)
        for part in (0, 1):
            send(0, way, part)
        load(1, way).start()
    for step in range(1, n):
        for way in (0, 1):
            load(step, way).wait()
            terms(way, fresh)
            if step + 1 < n:
                load(step + 1, way).start()
        for part in (0, 1):
            for way in (0, 1):
                made[step - 1, way, part].wait_recv()
                rows = parts[part]
                summed = landed[way, step - 1, rows].astype(jnp.float32) + fresh[way, rows].astype(
                    jnp.float32
                )
                if step == n - 1:
                    total[way, rows] = summed.astype(total.dtype)
                else:
                    landed[way, step - 1, rows] = summed.astype(landed.dtype)
                    send(step, way, part)
    for key in made:
        made[key].wait_send()


def ring_back(queries, grads, logs, deltas, slots):
    n, rows, _ = slots.shape
    return pl.pallas_call(
        lambda *refs: back_kernel(n, *refs),
        out_shape=(
            jax.ShapeDtypeStruct((2, rows, D), jnp.bfloat16),
            jax.ShapeDtypeStruct((HEADS // 2, 128, rows), jnp.float32),
        ),
        in_specs=[WHOLE, WHOLE, WHOLE, WHOLE, ANY],
        out_specs=(WHOLE, WHOLE),
        scratch_shapes=[
            pltpu.VMEM((2, n - 1, rows, D), jnp.bfloat16),
            pltpu.VMEM((2, rows, D), jnp.bfloat16),
            pltpu.VMEM((2, rows, D), jnp.bfloat16),
            pltpu.VMEM((2, rows, D), jnp.bfloat16),
            pltpu.SemaphoreType.DMA((2,)),
            pltpu.SemaphoreType.DMA((2, n - 1, 2)),
            pltpu.SemaphoreType.DMA((2, n - 1, 2)),
        ],
        cost_estimate=pl.CostEstimate(
            flops=80_000_000_000, bytes_accessed=2 * slots.size, transcendentals=0
        ),
        compiler_params=pltpu.CompilerParams(
            collective_id=2, has_side_effects=True, vmem_limit_bytes=67_000_000
        ),
        name="ring_back",
    )(queries, grads, logs, deltas, slots)


def sum_kernel(n, terms, total, landed, send_sem, recv_sem):
    ahead, behind = ring_neighbours()
    index = lax.axis_index("ctx")
    odd = index % 2
    place = (1 - odd) * (index // 2) + odd * (n - 1 - index // 2)
    greet((ahead, behind))

    def slot(way, back):
        return (place + n - back) % n if way == 0 else (place + back) % n

    rows = terms.shape[2]
    cut = 16 * (rows // 32)
    parts = (pl.ds(0, cut), pl.ds(cut, rows - cut))
    made = {}

    def send(source, target, step, way, part):
        copy = send_to(
            source,
            target,
            send_sem.at[way, step, part],
            recv_sem.at[way, step, part],
            (ahead, behind)[way],
        )
        copy.start()
        made[step, way, part] = copy

    both = [(part, way) for part in (0, 1) for way in (0, 1)]
    for part, way in both:
        piece = parts[part]
        send(terms.at[way, slot(way, 1), piece], landed.at[way, 0, piece], 0, way, part)
    for step in range(1, n):
        for part, way in both:
            piece = parts[part]
            made[step - 1, way, part].wait_recv()
            own = slot(way, step + 1)
            summed = (
                landed[way, step - 1, piece].astype(jnp.float32)
                + terms[way, own, piece].astype(jnp.float32)
            ).astype(landed.dtype)
            if step < n - 1:
                landed[way, step - 1, piece] = summed
                send(
                    landed.at[way, step - 1, piece], landed.at[way, step, piece], step, way, part
                )
            else:
                total[way, own, piece] = summed
                send(total.at[way, own, piece], total.at[way, own, piece], n - 1, way, part)
    for step in range(n, 2 * n - 2):
        for part, way in both:
            made[step - 1, way, part].wait_recv()
            have = slot(way, step - n + 1)
            piece = parts[part]
            send(total.at[way, have, piece], total.at[way, have, piece], step, way, part)
    for part, way in both:
        made[2 * n - 3, way, part].wait_recv()
    for key in made:
        made[key].wait_send()


def ring_sum(flat, ident):
    n = lax.axis_size("ctx")
    terms = flat.reshape(2, n, flat.size // (2 * n * 128), 128)
    rows = terms.shape[2]
    total = pl.pallas_call(
        lambda *refs: sum_kernel(n, *refs),
        out_shape=jax.ShapeDtypeStruct(terms.shape, terms.dtype),
        in_specs=[WHOLE],
        out_specs=WHOLE,
        scratch_shapes=[
            pltpu.VMEM((2, n - 1, rows, 128), terms.dtype),
            pltpu.SemaphoreType.DMA((2, 2 * n - 2, 2)),
            pltpu.SemaphoreType.DMA((2, 2 * n - 2, 2)),
        ],
        cost_estimate=pl.CostEstimate(
            flops=60_000_000_000, bytes_accessed=4 * terms.size, transcendentals=0
        ),
        compiler_params=pltpu.CompilerParams(collective_id=ident, has_side_effects=True),
        name="ring_sum",
    )(terms)
    return total.reshape(flat.shape)


def packed_terms(pieces, column):
    n = lax.axis_size("ctx")
    shards = lax.axis_size("fsdp")
    rows = pieces[0].shape[0]
    unit = 2 * n * 16 * 128
    width = sum(piece.shape[1] for piece in pieces) + 1
    step = 128
    while (rows // shards) * step % unit:
        step += 128
    full = -(-width // step) * step
    tail = jnp.pad(column.astype(jnp.bfloat16)[:, None], ((0, 0), (0, full - width)))
    return jnp.concatenate([piece.astype(jnp.bfloat16) for piece in pieces] + [tail], axis=1)


def on_device(
    inputs, cotangent, norm1_gain, qkv_weight, out_weight, norm2_gain, gate_up_weight, down_weight
):
    gains = jnp.pad(jnp.stack([norm1_gain, norm2_gain], axis=1), ((0, 0), (0, 126)))
    first = lax.all_gather(
        jnp.concatenate([qkv_weight, gains], axis=1), "fsdp", axis=0, tiled=True
    )
    w_qkv = first[:, : 3 * D]
    gain_one, gain_two = first[:, 3 * D], first[:, 3 * D + 1]
    w_out, w_gate_up, w_down = (
        lax.all_gather(out_weight, "fsdp", axis=0, tiled=True),
        lax.all_gather(gate_up_weight, "fsdp", axis=0, tiled=True),
        lax.all_gather(down_weight, "fsdp", axis=1, tiled=True),
    )
    local_rows = inputs.shape[1]
    first_row = lax.axis_index("ctx") * local_rows
    positions = (first_row + jnp.arange(local_rows, dtype=jnp.int32)).astype(jnp.float32)
    cosine_table, sine_table = rope_tables(positions)
    tokens = inputs[0].astype(jnp.float32)
    normed, norm_back = jax.vjp(layer_norm, tokens, gain_one.astype(jnp.float32))
    normed_low = normed.astype(jnp.bfloat16)
    projected = jnp.dot(normed_low, w_qkv, preferred_element_type=jnp.float32)
    rotated, rope_back = jax.vjp(
        lambda values: split_rope(values, cosine_table, sine_table), projected
    )
    queries = rotated[0].astype(jnp.bfloat16).reshape(local_rows, D)
    key_rows = rotated[1].astype(jnp.bfloat16).reshape(local_rows, D)
    value_rows = rotated[2].astype(jnp.bfloat16).reshape(local_rows, D)
    cut = D // 2
    block = jnp.concatenate(
        [key_rows[:, :cut], value_rows[:, :cut], key_rows[:, cut:], value_rows[:, cut:]], axis=1
    )
    slots, attended, log_total = ring_attend(block, queries)
    attended_low = attended.astype(jnp.bfloat16)
    middle = tokens + jnp.dot(attended_low, w_out, preferred_element_type=jnp.float32)
    normed_two, norm_back_two = jax.vjp(layer_norm, middle, gain_two.astype(jnp.float32))
    normed_two_low = normed_two.astype(jnp.bfloat16)
    gate_up = jnp.dot(normed_two_low, w_gate_up, preferred_element_type=jnp.float32)
    hidden, geglu_back = jax.vjp(geglu, gate_up)
    hidden_low = hidden.astype(jnp.bfloat16)
    output = (middle + jnp.dot(hidden_low, w_down, preferred_element_type=jnp.float32)).astype(
        jnp.bfloat16
    )
    upstream = cotangent[0]
    grad_down = jnp.einsum("lf,ld->df", hidden_low, upstream, preferred_element_type=jnp.float32)
    grad_hidden = jnp.einsum("ld,fd->lf", upstream, w_down, preferred_element_type=jnp.float32)
    grad_gate_up = geglu_back(grad_hidden)[0].astype(jnp.bfloat16)
    grad_w_gate_up = jnp.einsum(
        "ld,lf->df", normed_two_low, grad_gate_up, preferred_element_type=jnp.float32
    )
    grad_normed_two = jnp.einsum(
        "lf,df->ld", grad_gate_up, w_gate_up, preferred_element_type=jnp.float32
    )
    grad_middle_part, grad_gain_two = norm_back_two(grad_normed_two)
    grad_middle = upstream.astype(jnp.float32) + grad_middle_part
    grad_branch = grad_middle.astype(jnp.bfloat16)
    grad_w_out = jnp.einsum(
        "ld,le->de", attended_low, grad_branch, preferred_element_type=jnp.float32
    )
    grad_attended = jnp.einsum(
        "le,de->ld", grad_branch, w_out, preferred_element_type=jnp.float32
    ).astype(jnp.bfloat16)
    deltas = jnp.sum(
        heads_of(grad_attended.astype(jnp.float32) * attended), axis=-1
    ).T[:, None, :]
    packed_one = packed_terms((grad_w_gate_up, grad_down, grad_w_out), grad_gain_two)
    packed_one, grad_attended, deltas = lax.optimization_barrier(
        (packed_one, grad_attended, deltas)
    )
    shard_one = lax.psum_scatter(packed_one, "fsdp", scatter_dimension=0, tiled=True)
    grad_kv, grad_query_t = ring_back(queries, grad_attended, log_total, deltas, slots)
    shard_one, grad_kv, grad_query_t = lax.optimization_barrier(
        (shard_one, grad_kv, grad_query_t)
    )
    grad_query = grad_query_t.reshape(D, local_rows).T
    grad_key = jnp.concatenate([grad_kv[0, :, :cut], grad_kv[1, :, :cut]], axis=1)
    grad_value = jnp.concatenate([grad_kv[0, :, cut:], grad_kv[1, :, cut:]], axis=1)
    grad_rotated = (
        rounded(heads_of(grad_query)),
        heads_of(grad_key.astype(jnp.float32)),
        heads_of(grad_value.astype(jnp.float32)),
    )
    grad_projected = rope_back(grad_rotated)[0].astype(jnp.bfloat16)
    grad_w_qkv = jnp.einsum(
        "ld,lf->df", normed_low, grad_projected, preferred_element_type=jnp.float32
    )
    grad_normed = jnp.einsum("lf,df->ld", grad_projected, w_qkv, preferred_element_type=jnp.float32)
    grad_tokens_part, grad_gain_one = norm_back(grad_normed)
    input_grad = grad_middle + grad_tokens_part
    shard_one, packed_two = lax.optimization_barrier(
        (shard_one, packed_terms((grad_w_qkv,), grad_gain_one))
    )
    shard_two = lax.psum_scatter(packed_two, "fsdp", scatter_dimension=0, tiled=True)
    total_one = ring_sum(shard_one, 3).astype(jnp.float32)
    total_two = ring_sum(shard_two, 4).astype(jnp.float32)
    up_end, down_end, out_end = 2 * FF, 3 * FF, 3 * FF + D
    return (
        output[None],
        input_grad[None],
        total_two[:, 3 * D],
        total_one[:, out_end],
        total_two[:, : 3 * D],
        total_one[:, down_end:out_end],
        total_one[:, :up_end],
        total_one[:, up_end:down_end].T,
    )


def solution(mesh):
    in_specs = (
        P("fsdp", "ctx", None),
        P("fsdp", "ctx", None),
        P("fsdp"),
        P("fsdp", None),
        P("fsdp", None),
        P("fsdp"),
        P("fsdp", None),
        P(None, "fsdp"),
    )
    out_specs = (
        P("fsdp", "ctx", None),
        P("fsdp", "ctx", None),
        P("fsdp"),
        P("fsdp"),
        P("fsdp", None),
        P("fsdp", None),
        P("fsdp", None),
        P(None, "fsdp"),
    )
    return jax.shard_map(
        on_device, mesh=mesh, in_specs=in_specs, out_specs=out_specs, check_vma=False
    )
```
